32 devices in a mesh: groups: 2 (over y), row: 8 (over z, x), col: 2 (over core).
Axes of the slice: x: 2, y: 2, z: 4, core: 2. Of those that a mesh axis runs over, the one named last changes fastest.
Arguments:
- sigma_anc: bfloat16 [16384, 8192], P(('groups', 'row'), 'col'), parts along dimension 0, as said below
- panel: bfloat16 [16384, 3072], P(('groups', 'row'), 'col'), parts along dimension 0
- holder: int32 [128], P('groups'), parts along dimension 0, may hold values from 0 to 63, each once
- dinv_diag: float32 [6144], P(('groups', 'col')), parts along dimension 0, may hold values from 0.5 to 2
Outputs:
- sigma_aj: bfloat16 [16384, 3072], P(('groups', 'row'), 'col'), parts along dimension 0
- variances: float32 [6144], P(('groups', 'col')), parts along dimension 0
The draws below stay inside these ranges and needn't reach their ends.
There are 2 independent parts, one for each index of `groups`. The reference program is written for one: setup_inputs(seed, part) draws one part's arguments, and reference() takes and returns one part's arrays. A program takes and returns all parts, laid end to end along the dimension named above; each array names one. Nothing has to cross between parts.
Inputs may be any that keep to these rules, and one draw needn't show every extreme that they name: holder is a permutation of the 64 tiles. sigma_anc is symmetric and positive definite.
All inputs are finite; a program needn't handle non-finite values.
Results may differ from the reference program's by a relative error of at most 0.001.
Values may be sent and summed in bfloat16 or wider, within the bound.
A program may use at most 128 MiB of HBM per device.

```python
import math
import jax
import jax.numpy as jnp

A = 8192
S = 3072
TILE = 128
TILES = 64


def draw_sigma_anc(key, part):
    kone = jax.random.fold_in(key, 11)
    ktwo = jax.random.fold_in(key, 12)
    base = jax.random.normal(kone, (A, A), jnp.float32)
    sym = (base + base.T) * (0.5 / jnp.sqrt(jnp.float32(A)))
    diag = jax.random.uniform(ktwo, (A,), jnp.float32, 1.5, 3.0)
    return (sym + jnp.diag(diag)).astype(jnp.bfloat16)


def draw_panel(key, part):
    kone = jax.random.fold_in(key, 21)
    ktwo = jax.random.fold_in(key, 22)
    rows = jnp.arange(A, dtype=jnp.float32) / A
    row_scale = 10.0 ** (rows - 0.5)
    col_scale = 10.0 ** jax.random.uniform(ktwo, (S,), jnp.float32, -0.5, 0.5)
    entries = jax.random.normal(kone, (A, S), jnp.float32)
    vals = entries * row_scale[:, None] * col_scale[None, :] / jnp.sqrt(jnp.float32(A))
    return vals.astype(jnp.bfloat16)


def block_levels(stream_key, shape, split, least, largest):
    def one(position, parts):
        heights = jax.random.uniform(jax.random.fold_in(jax.random.fold_in(stream_key, 6), position), (parts,), jnp.float32, least / len(split), largest / len(split))
        return jnp.repeat(jnp.exp(heights), shape[position] // parts).reshape((-1,) + (1,) * (len(shape) - position - 1))

    loudness = one(*split[0])
    for cut in split[1:]:
        loudness = loudness * one(*cut)
    return loudness


def setup_inputs(seed: int = 0, part: int = 0) -> dict:
    key_of = jax.random.split(jax.random.key(seed), 5)
    part_keys = jax.random.split(jax.random.fold_in(key_of[4], part), 5)
    return {
        "sigma_anc": draw_sigma_anc(jax.random.fold_in(jax.random.fold_in(key_of[4], part), 71), part),
        "panel": draw_panel(jax.random.fold_in(jax.random.fold_in(key_of[4], part), 71), part),
        "holder": jax.random.permutation(part_keys[2], TILES).astype(jnp.int32),
        "dinv_diag": jnp.clip(jnp.exp(math.log(2.0) - 1.3862944 * jax.random.uniform(part_keys[3], (S,), jnp.float32) ** block_levels(part_keys[3], (S,), ((0, 2),), -0.2, 0.2)), 0.5, 2.0),
    }


def reference(sigma_anc, panel, holder, dinv_diag):
    tiles = panel.reshape(TILES, TILE, S)
    panel_log = jnp.take(tiles, holder.astype(jnp.int32), axis=0).reshape(A, S)
    prod = jnp.dot(sigma_anc, panel_log, preferred_element_type=jnp.float32)
    sigma_aj = (-prod).astype(jnp.bfloat16)
    variances = dinv_diag + jnp.sum(panel_log.astype(jnp.float32) * prod, axis=0)
    return sigma_aj, variances
```

```python
import functools

import jax
import jax.numpy as jnp
from jax import lax
from jax.experimental import pallas as pl
from jax.experimental.pallas import tpu as pltpu
from jax.sharding import PartitionSpec as P

MESH = pl.DeviceIdType.MESH


def block_of(size, most):
    block = min(size, most)
    while size % block:
        block -= 128
    return block


def kernel(n, nc, holder, logical, sigma, panel, out, sums, s, p, acc, staged, parts,
           own_sem, far_sem, near_sem, f_send, f_recv, b_send, b_recv, o_sem, v_send, v_recv):
    g = lax.axis_index("groups")
    r = lax.axis_index("row")
    c = lax.axis_index("col")
    per, tile, cols = panel.shape
    rows, width = sigma.shape
    tiles = p.shape[0]
    half = n // 2
    fwd = (per + 1) // 2
    bwd = per - fwd

    def row_of(at):
        at = lax.rem(at + 2 * n, n)
        odd = at // half
        return 2 * (at + odd * (2 * half - 1 - 2 * at)) + odd

    odd = lax.rem(r, 2)
    up = r // 2
    at = up + odd * (2 * half - 1 - 2 * up)
    after = (g, row_of(at + 1), c)
    before = (g, row_of(at - 1), c)

    barrier = pltpu.get_barrier_semaphore()

    def greet(k, carry):
        pl.semaphore_signal(barrier, 1, device_id=(g, lax.rem(r + k, n), c), device_id_type=MESH)
        return carry

    lax.fori_loop(1, n, greet, 0)
    for k in range(1, nc):
        pl.semaphore_signal(barrier, 1, device_id=(g, r, lax.rem(c + k, nc)), device_id_type=MESH)
    pl.semaphore_wait(barrier, n - 1 + nc - 1)

    def f_tile(k, i):
        return row_of(at - k) * per + i

    def b_tile(k, i):
        return row_of(at + k) * per + fwd + i

    def f_copy(k, i, src=None):
        t = f_tile(k, i)
        return pltpu.make_async_remote_copy(
            src_ref=p.at[t] if src is None else src, dst_ref=p.at[t],
            send_sem=f_send.at[k * fwd + i], recv_sem=f_recv.at[k * fwd + i],
            device_id=after, device_id_type=MESH)

    def b_copy(k, i, src=None):
        t = b_tile(k, i)
        return pltpu.make_async_remote_copy(
            src_ref=p.at[t] if src is None else src, dst_ref=p.at[t],
            send_sem=b_send.at[k * bwd + i], recv_sem=b_recv.at[k * bwd + i],
            device_id=before, device_id_type=MESH)

    def f_landed(k, i):
        t = f_tile(k, i)
        return pltpu.make_async_remote_copy(
            src_ref=p.at[t], dst_ref=p.at[t],
            send_sem=f_send.at[(k - 1) * fwd + i], recv_sem=f_recv.at[(k - 1) * fwd + i],
            device_id=after, device_id_type=MESH)

    def b_landed(k, i):
        t = b_tile(k, i)
        return pltpu.make_async_remote_copy(
            src_ref=p.at[t], dst_ref=p.at[t],
            send_sem=b_send.at[(k - 1) * bwd + i], recv_sem=b_recv.at[(k - 1) * bwd + i],
            device_id=before, device_id_type=MESH)

    for i in range(fwd):
        f_copy(0, i, panel.at[i]).start()
        if i < bwd:
            b_copy(0, i, panel.at[fwd + i]).start()

    held = width // tile

    def near(j):
        return pltpu.make_async_copy(
            sigma.at[:, pl.ds(pl.multiple_of(j * tile, tile), tile)], s.at[c * held + j], near_sem.at[j])

    def far(k, j):
        return pltpu.make_async_remote_copy(
            src_ref=sigma.at[:, pl.ds(pl.multiple_of(j * tile, tile), tile)], dst_ref=s.at[c * held + j],
            send_sem=far_sem.at[2 * k - 2, j], recv_sem=far_sem.at[2 * k - 1, j],
            device_id=(g, r, lax.rem(c + k, nc)), device_id_type=MESH)

    def far_landed(k, j):
        t = lax.rem(c + nc - k, nc) * held + j
        return pltpu.make_async_remote_copy(
            src_ref=s.at[t], dst_ref=s.at[t],
            send_sem=far_sem.at[2 * k - 2, j], recv_sem=far_sem.at[2 * k - 1, j],
            device_id=(g, r, lax.rem(c + k, nc)), device_id_type=MESH)

    def each(low, high, act):
        def step(k, carry):
            act(k)
            return carry
        lax.fori_loop(low, high, step, 0)

    for k in range(1, nc):
        each(0, held, lambda j: far(k, j).start())
    each(0, held, lambda j: near(j).start())
    own = pltpu.make_async_copy(panel, p.at[pl.ds(r * per, per)], own_sem)
    own.start()
    acc[...] = jnp.zeros_like(acc)
    own.wait()
    each(0, held, lambda j: near(j).wait())
    for k in range(1, nc):
        each(0, held, lambda j: far_landed(k, j).wait_recv())

    rb = block_of(rows, 512)
    cb = block_of(cols, 512)
    across = cols // cb

    def multiply(slots):
        columns = [logical[t] for t in slots]

        def block(q, carry):
            rs = pl.ds(pl.multiple_of((q // across) * rb, rb), rb)
            cs = pl.ds(pl.multiple_of(lax.rem(q, across) * cb, cb), cb)
            lhs = jnp.concatenate([s[w, rs, :] for w in columns], axis=1)
            rhs = jnp.concatenate([p[t, :, cs] for t in slots], axis=0)
            acc[rs, cs] += jnp.dot(lhs, rhs, preferred_element_type=jnp.float32)
            return carry

        lax.fori_loop(0, (rows // rb) * across, block, 0)

    def unit(u, carry):
        k = u // fwd
        i = lax.rem(u, fwd)

        @pl.when(k > 0)
        def _():
            f_landed(k, i).wait_recv()

            @pl.when(k < n - 1)
            def _():
                f_copy(k, i).start()

        if bwd == fwd:
            @pl.when(k > 0)
            def _():
                b_landed(k, i).wait_recv()

                @pl.when(k < n - 1)
                def _():
                    b_copy(k, i).start()

            multiply([f_tile(k, i), b_tile(k, i)])
        else:
            multiply([f_tile(k, i)])
            if bwd:
                @pl.when(i < bwd)
                def _():
                    @pl.when(k > 0)
                    def _():
                        b_landed(k, i).wait_recv()

                        @pl.when(k < n - 1)
                        def _():
                            b_copy(k, i).start()

                    multiply([b_tile(k, i)])
        return carry

    lax.fori_loop(0, n * fwd, unit, 0)

    def put(j):
        where = pl.ds(pl.multiple_of(j * tile, tile), tile)
        return pltpu.make_async_copy(staged.at[where], out.at[where], o_sem.at[j])

    parts[r] = jnp.zeros((1, cols), jnp.float32)

    def finish(j, carry):
        where = pl.ds(pl.multiple_of(j * tile, tile), tile)
        mine = p[holder[r * per + j]]
        for b in range(across):
            cs = pl.ds(b * cb, cb)
            prod = acc[where, cs]
            staged[where, cs] = (-prod).astype(staged.dtype)
            term = mine[:, b * cb:(b + 1) * cb].astype(jnp.float32) * prod
            parts[r, :, cs] += jnp.sum(term, axis=0, keepdims=True)
        put(j).start()
        return carry

    lax.fori_loop(0, per, finish, 0)

    def share(k):
        to = lax.rem(r + k, n)
        return pltpu.make_async_remote_copy(
            src_ref=parts.at[r], dst_ref=parts.at[r],
            send_sem=v_send.at[k - 1], recv_sem=v_recv.at[k - 1],
            device_id=(g, to, c), device_id_type=MESH)

    def gone(k):
        frm = lax.rem(r + n - k, n)
        return pltpu.make_async_remote_copy(
            src_ref=parts.at[frm], dst_ref=parts.at[frm],
            send_sem=v_send.at[k - 1], recv_sem=v_recv.at[k - 1],
            device_id=(g, lax.rem(r + k, n), c), device_id_type=MESH)

    each(1, n, lambda k: share(k).start())
    for k in range(1, nc):
        each(0, held, lambda j: far(k, j).wait_send())
    each(0, (n - 1) * fwd, lambda u: f_copy(u // fwd, lax.rem(u, fwd)).wait_send())
    if bwd:
        each(0, (n - 1) * bwd, lambda u: b_copy(u // bwd, lax.rem(u, bwd)).wait_send())
    each(0, per, lambda j: put(j).wait())
    each(1, n, lambda k: gone(k).wait_recv())
    each(1, n, lambda k: share(k).wait_send())
    total = parts[0]
    for k in range(1, n):
        total += parts[k]
    sums[...] = total


def body(n, nc, sigma_anc, panel, holder, dinv_diag):
    tiles = holder.shape[0]
    rows, width = sigma_anc.shape
    cols = panel.shape[1]
    per = tiles // n
    tile = panel.shape[0] // per
    fwd = (per + 1) // 2
    bwd = max(per - fwd, 1)
    ids = jnp.arange(tiles, dtype=jnp.int32)
    logical = jnp.sum(jnp.where(holder[:, None] == ids[None, :], ids[:, None], 0), axis=0, dtype=jnp.int32)
    dma = pltpu.SemaphoreType.DMA
    out, sums = pl.pallas_call(
        functools.partial(kernel, n, nc),
        out_shape=(
            jax.ShapeDtypeStruct((rows, cols), jnp.bfloat16),
            jax.ShapeDtypeStruct((1, cols), jnp.float32),
        ),
        in_specs=[
            pl.BlockSpec(memory_space=pltpu.SMEM),
            pl.BlockSpec(memory_space=pltpu.SMEM),
            pl.BlockSpec(memory_space=pl.ANY),
            pl.BlockSpec(memory_space=pl.ANY),
        ],
        out_specs=(
            pl.BlockSpec(memory_space=pl.ANY),
            pl.BlockSpec(memory_space=pltpu.VMEM),
        ),
        scratch_shapes=[
            pltpu.VMEM((width * nc // tile, rows, tile), sigma_anc.dtype),
            pltpu.VMEM((tiles, tile, cols), panel.dtype),
            pltpu.VMEM((rows, cols), jnp.float32),
            pltpu.VMEM((rows, cols), jnp.bfloat16),
            pltpu.VMEM((n, 1, cols), jnp.float32),
            dma,
            dma((2 * nc, width // tile)),
            dma((width // tile,)),
            dma((n * fwd,)),
            dma((n * fwd,)),
            dma((n * bwd,)),
            dma((n * bwd,)),
            dma((per,)),
            dma((n,)),
            dma((n,)),
        ],
        compiler_params=pltpu.CompilerParams(
            collective_id=0, has_side_effects=True, vmem_limit_bytes=60 << 20
        ),
    )(holder, logical, sigma_anc, panel.reshape(per, tile, cols))
    return out, dinv_diag + sums.reshape(cols)


def solution(mesh):
    placed = (
        P(("groups", "row"), "col"),
        P(("groups", "row"), "col"),
        P("groups"),
        P(("groups", "col")),
    )
    return jax.shard_map(
        functools.partial(body, mesh.shape["row"], mesh.shape["col"]),
        mesh=mesh,
        in_specs=placed,
        out_specs=(P(("groups", "row"), "col"), P(("groups", "col"))),
        check_vma=False,
    )
```

```python
import functools

import jax
import jax.numpy as jnp
from jax import lax
from jax.experimental import pallas as pl
from jax.experimental.pallas import tpu as pltpu
from jax.sharding import PartitionSpec as P

MESH = pl.DeviceIdType.MESH


def block_of(size, most):
    block = min(size, most)
    while size % block:
        block -= 128
    return block


def kernel(n, nc, holder, logical, sigma, panel, out, sums, s, p, acc, staged, parts,
           own_sem, far_sem, near_sem, f_send, f_recv, b_send, b_recv, o_sem, v_send, v_recv):
    g = lax.axis_index("groups")
    r = lax.axis_index("row")
    c = lax.axis_index("col")
    per, tile, cols = panel.shape
    rows, width = sigma.shape
    tiles = p.shape[0]
    half = n // 2
    fwd = (per + 1) // 2
    bwd = per - fwd

    def row_of(at):
        at = lax.rem(at + 2 * n, n)
        odd = at // half
        return 2 * (at + odd * (2 * half - 1 - 2 * at)) + odd

    odd = lax.rem(r, 2)
    up = r // 2
    at = up + odd * (2 * half - 1 - 2 * up)
    after = (g, row_of(at + 1), c)
    before = (g, row_of(at - 1), c)

    barrier = pltpu.get_barrier_semaphore()

    def greet(k, carry):
        pl.semaphore_signal(barrier, 1, device_id=(g, lax.rem(r + k, n), c), device_id_type=MESH)
        return carry

    lax.fori_loop(1, n, greet, 0)
    for k in range(1, nc):
        pl.semaphore_signal(barrier, 1, device_id=(g, r, lax.rem(c + k, nc)), device_id_type=MESH)
    pl.semaphore_wait(barrier, n - 1 + nc - 1)

    def f_tile(k, i):
        return row_of(at - k) * per + i

    def b_tile(k, i):
        return row_of(at + k) * per + fwd + i

    def f_copy(k, i, src=None):
        t = f_tile(k, i)
        return pltpu.make_async_remote_copy(
            src_ref=p.at[t] if src is None else src, dst_ref=p.at[t],
            send_sem=f_send.at[k * fwd + i], recv_sem=f_recv.at[k * fwd + i],
            device_id=after, device_id_type=MESH)

    def b_copy(k, i, src=None):
        t = b_tile(k, i)
        return pltpu.make_async_remote_copy(
            src_ref=p.at[t] if src is None else src, dst_ref=p.at[t],
            send_sem=b_send.at[k * bwd + i], recv_sem=b_recv.at[k * bwd + i],
            device_id=before, device_id_type=MESH)

    def f_landed(k, i):
        t = f_tile(k, i)
        return pltpu.make_async_remote_copy(
            src_ref=p.at[t], dst_ref=p.at[t],
            send_sem=f_send.at[(k - 1) * fwd + i], recv_sem=f_recv.at[(k - 1) * fwd + i],
            device_id=after, device_id_type=MESH)

    def b_landed(k, i):
        t = b_tile(k, i)
        return pltpu.make_async_remote_copy(
            src_ref=p.at[t], dst_ref=p.at[t],
            send_sem=b_send.at[(k - 1) * bwd + i], recv_sem=b_recv.at[(k - 1) * bwd + i],
            device_id=before, device_id_type=MESH)

    for i in range(fwd):
        f_copy(0, i, panel.at[i]).start()
        if i < bwd:
            b_copy(0, i, panel.at[fwd + i]).start()

    held = width // tile

    def near(j):
        return pltpu.make_async_copy(
            sigma.at[:, pl.ds(pl.multiple_of(j * tile, tile), tile)], s.at[c * held + j], near_sem.at[j])

    def far(k, j):
        return pltpu.make_async_remote_copy(
            src_ref=sigma.at[:, pl.ds(pl.multiple_of(j * tile, tile), tile)], dst_ref=s.at[c * held + j],
            send_sem=far_sem.at[2 * k - 2, j], recv_sem=far_sem.at[2 * k - 1, j],
            device_id=(g, r, lax.rem(c + k, nc)), device_id_type=MESH)

    def far_landed(k, j):
        t = lax.rem(c + nc - k, nc) * held + j
        return pltpu.make_async_remote_copy(
            src_ref=s.at[t], dst_ref=s.at[t],
            send_sem=far_sem.at[2 * k - 2, j], recv_sem=far_sem.at[2 * k - 1, j],
            device_id=(g, r, lax.rem(c + k, nc)), device_id_type=MESH)

    def each(low, high, act):
        def step(k, carry):
            act(k)
            return carry
        lax.fori_loop(low, high, step, 0)

    for k in range(1, nc):
        each(0, held, lambda j: far(k, j).start())
    each(0, held, lambda j: near(j).start())
    own = pltpu.make_async_copy(panel, p.at[pl.ds(r * per, per)], own_sem)
    own.start()
    acc[...] = jnp.zeros_like(acc)
    own.wait()
    each(0, held, lambda j: near(j).wait())
    for k in range(1, nc):
        each(0, held, lambda j: far_landed(k, j).wait_recv())

    rb = block_of(rows, 512)
    cb = block_of(cols, 512)
    across = cols // cb

    def multiply(slots):
        columns = [logical[t] for t in slots]

        def block(q, carry):
            rs = pl.ds(pl.multiple_of((q // across) * rb, rb), rb)
            cs = pl.ds(pl.multiple_of(lax.rem(q, across) * cb, cb), cb)
            lhs = jnp.concatenate([s[w, rs, :] for w in columns], axis=1)
            rhs = jnp.concatenate([p[t, :, cs] for t in slots], axis=0)
            acc[rs, cs] += jnp.dot(lhs, rhs, preferred_element_type=jnp.float32)
            return carry

        lax.fori_loop(0, (rows // rb) * across, block, 0)

    def unit(u, carry):
        k = u // fwd
        i = lax.rem(u, fwd)

        @pl.when(k > 0)
        def _():
            f_landed(k, i).wait_recv()

            @pl.when(k < n - 1)
            def _():
                f_copy(k, i).start()

        if bwd == fwd:
            @pl.when(k > 0)
            def _():
                b_landed(k, i).wait_recv()

                @pl.when(k < n - 1)
                def _():
                    b_copy(k, i).start()

            multiply([f_tile(k, i), b_tile(k, i)])
        else:
            multiply([f_tile(k, i)])
            if bwd:
                @pl.when(i < bwd)
                def _():
                    @pl.when(k > 0)
                    def _():
                        b_landed(k, i).wait_recv()

                        @pl.when(k < n - 1)
                        def _():
                            b_copy(k, i).start()

                    multiply([b_tile(k, i)])
        return carry

    lax.fori_loop(0, n * fwd, unit, 0)

    parts[r] = jnp.zeros((1, cols), jnp.float32)

    def weigh(j, carry):
        where = pl.ds(pl.multiple_of(j * tile, tile), tile)
        mine = p[holder[r * per + j]]
        for b in range(across):
            cs = pl.ds(b * cb, cb)
            term = mine[:, b * cb:(b + 1) * cb].astype(jnp.float32) * acc[where, cs]
            parts[r, :, cs] += jnp.sum(term, axis=0, keepdims=True)
        return carry

    lax.fori_loop(0, per, weigh, 0)

    def share(k):
        to = lax.rem(r + k, n)
        return pltpu.make_async_remote_copy(
            src_ref=parts.at[r], dst_ref=parts.at[r],
            send_sem=v_send.at[k - 1], recv_sem=v_recv.at[k - 1],
            device_id=(g, to, c), device_id_type=MESH)

    def gone(k):
        frm = lax.rem(r + n - k, n)
        return pltpu.make_async_remote_copy(
            src_ref=parts.at[frm], dst_ref=parts.at[frm],
            send_sem=v_send.at[k - 1], recv_sem=v_recv.at[k - 1],
            device_id=(g, lax.rem(r + k, n), c), device_id_type=MESH)

    each(1, n, lambda k: share(k).start())

    def put(j):
        where = pl.ds(pl.multiple_of(j * tile, tile), tile)
        return pltpu.make_async_copy(staged.at[where], out.at[where], o_sem.at[j])

    def finish(j, carry):
        where = pl.ds(pl.multiple_of(j * tile, tile), tile)
        staged[where, :] = (-acc[where, :]).astype(staged.dtype)
        put(j).start()
        return carry

    lax.fori_loop(0, per, finish, 0)

    for k in range(1, nc):
        each(0, held, lambda j: far(k, j).wait_send())
    each(0, (n - 1) * fwd, lambda u: f_copy(u // fwd, lax.rem(u, fwd)).wait_send())
    if bwd:
        each(0, (n - 1) * bwd, lambda u: b_copy(u // bwd, lax.rem(u, bwd)).wait_send())
    each(0, per, lambda j: put(j).wait())
    each(1, n, lambda k: gone(k).wait_recv())
    each(1, n, lambda k: share(k).wait_send())
    total = parts[0]
    for k in range(1, n):
        total += parts[k]
    sums[...] = total


def body(n, nc, sigma_anc, panel, holder, dinv_diag):
    tiles = holder.shape[0]
    rows, width = sigma_anc.shape
    cols = panel.shape[1]
    per = tiles // n
    tile = panel.shape[0] // per
    fwd = (per + 1) // 2
    bwd = max(per - fwd, 1)
    ids = jnp.arange(tiles, dtype=jnp.int32)
    logical = jnp.sum(jnp.where(holder[:, None] == ids[None, :], ids[:, None], 0), axis=0, dtype=jnp.int32)
    dma = pltpu.SemaphoreType.DMA
    out, sums = pl.pallas_call(
        functools.partial(kernel, n, nc),
        out_shape=(
            jax.ShapeDtypeStruct((rows, cols), jnp.bfloat16),
            jax.ShapeDtypeStruct((1, cols), jnp.float32),
        ),
        in_specs=[
            pl.BlockSpec(memory_space=pltpu.SMEM),
            pl.BlockSpec(memory_space=pltpu.SMEM),
            pl.BlockSpec(memory_space=pl.ANY),
            pl.BlockSpec(memory_space=pl.ANY),
        ],
        out_specs=(
            pl.BlockSpec(memory_space=pl.ANY),
            pl.BlockSpec(memory_space=pltpu.VMEM),
        ),
        scratch_shapes=[
            pltpu.VMEM((width * nc // tile, rows, tile), sigma_anc.dtype),
            pltpu.VMEM((tiles, tile, cols), panel.dtype),
            pltpu.VMEM((rows, cols), jnp.float32),
            pltpu.VMEM((rows, cols), jnp.bfloat16),
            pltpu.VMEM((n, 1, cols), jnp.float32),
            dma,
            dma((2 * nc, width // tile)),
            dma((width // tile,)),
            dma((n * fwd,)),
            dma((n * fwd,)),
            dma((n * bwd,)),
            dma((n * bwd,)),
            dma((per,)),
            dma((n,)),
            dma((n,)),
        ],
        compiler_params=pltpu.CompilerParams(
            collective_id=0, has_side_effects=True, vmem_limit_bytes=60 << 20
        ),
    )(holder, logical, sigma_anc, panel.reshape(per, tile, cols))
    return out, dinv_diag + sums.reshape(cols)


def solution(mesh):
    placed = (
        P(("groups", "row"), "col"),
        P(("groups", "row"), "col"),
        P("groups"),
        P(("groups", "col")),
    )
    return jax.shard_map(
        functools.partial(body, mesh.shape["row"], mesh.shape["col"]),
        mesh=mesh,
        in_specs=placed,
        out_specs=(P(("groups", "row"), "col"), P(("groups", "col"))),
        check_vma=False,
    )
```
